32 devices in a mesh: groups: 2 (over x), frame: 16 (over z, y, core).
Axes of the slice: x: 2, y: 2, z: 4, core: 2. Of those that a mesh axis runs over, the one named last changes fastest.
Arguments:
- latent_images: bfloat16 [64, 4, 240, 256], P(('groups', 'frame')), parts along dimension 0, may hold values from -6 to 6
- initial_group_scale: float32 [256], replicated, may hold values from 0.1 to 1.9
- initial_conv_taps: bfloat16 [3, 3, 256, 256], replicated, may hold values from -0.125 to 0.125
- later_group_scale: float32 [256], replicated, may hold values from 0.1 to 1.9
- later_conv_taps: bfloat16 [3, 3, 256, 256], replicated, may hold values from -0.125 to 0.125
- prenormal_scale_vector: float32 [256], replicated, may hold values from 0.1 to 1.9
- asking_projection_matrix: bfloat16 [256, 256], replicated, may hold values from -0.375 to 0.375
- matching_projection_matrix: bfloat16 [256, 256], replicated, may hold values from -0.375 to 0.375
- content_projection_matrix: bfloat16 [256, 256], replicated, may hold values from -0.375 to 0.375
- closing_projection_matrix: bfloat16 [256, 256], replicated, may hold values from -0.375 to 0.375
- neighbour_time_taps: bfloat16 [3, 256, 256], replicated, may hold values from -0.21875 to 0.21875
- score_sharpness: float32 [4], replicated, may hold values from 0.5 to 120
Outputs:
- result: bfloat16 [64, 4, 240, 256], P(('groups', 'frame')), parts along dimension 0
The draws below stay inside these ranges and needn't reach their ends.
There are 2 independent parts, one for each index of `groups`. The reference program is written for one: setup_inputs(seed, part) draws one part's arguments, and reference() takes and returns one part's arrays. A program takes and returns all parts, laid end to end along the dimension named above; an argument that names none is the same for every part. Nothing has to cross between parts.
All inputs are finite; a program needn't handle non-finite values.
Results may differ from the reference program's by a relative error of at most 0.022.
The reference program's roundings to bfloat16 on the way count: a program that leaves them out, or rounds other values in their place, can miss the bound.
Values may be sent and summed in bfloat16 or wider, within the bound.
A program may use at most 64 MiB of HBM per device.

```python
import math
import jax
import jax.numpy as jnp
from jax import lax

C = 256
HEADS = 4
GROUPS = 32
HT = 4
W = 240
FRAMES = 32
OWN = 60
N_FRAME = 16


def draw_score_sharpness(key, part):
    logs = jax.random.uniform(key, (HEADS,), jnp.float32, math.log(0.5), math.log(2.0))
    return jnp.exp(logs)


def block_levels(rng, dims, pieces, smallest, top_value):
    loudness, own = 1.0, jax.random.fold_in(rng, 6)
    for dim, shards_of in pieces:
        draws = jnp.exp(jax.random.uniform(jax.random.fold_in(own, dim), (shards_of,), jnp.float32, smallest / len(pieces), top_value / len(pieces)))
        loudness = loudness * jnp.repeat(draws, dims[dim] // shards_of).reshape([-1 if axis == dim else 1 for axis in range(len(dims))])
    return loudness


def centred(stream_key, shape, deviation, limit, shards=(), dtype=jnp.bfloat16):
    loudness = block_levels(stream_key, shape, shards, -0.22, 0.18) if shards else 1.0
    array = jax.random.normal(stream_key, shape, jnp.float32) * deviation * loudness
    return jnp.minimum(jnp.maximum(array, -limit), limit).astype(dtype)


def setup_inputs(seed: int = 0, part: int = 0) -> dict:
    streams_of = jax.random.split(jax.random.key(seed), 13)
    part_keys = jax.random.split(jax.random.fold_in(streams_of[12], part), 13)
    return {
        "latent_images": centred(part_keys[0], (FRAMES, HT, W, C), 1.0, 6.0, ((0, 16),)),
        "initial_group_scale": jnp.clip(1.0 + 0.18 * jax.random.normal(streams_of[1], (C,), jnp.float32), 0.1, 1.9),
        "initial_conv_taps": centred(streams_of[2], (3, 3, C, C), (9 * C) ** -0.5, 0.125),
        "later_group_scale": jnp.clip(1.0 + 0.18 * jax.random.normal(streams_of[3], (C,), jnp.float32), 0.1, 1.9),
        "later_conv_taps": centred(streams_of[4], (3, 3, C, C), (9 * C) ** -0.5, 0.125),
        "prenormal_scale_vector": jnp.clip(1.0 + 0.18 * jax.random.normal(streams_of[5], (C,), jnp.float32), 0.1, 1.9),
        "asking_projection_matrix": centred(streams_of[6], (C, C), C ** -0.5, 0.375),
        "matching_projection_matrix": centred(streams_of[7], (C, C), C ** -0.5, 0.375),
        "content_projection_matrix": centred(streams_of[8], (C, C), C ** -0.5, 0.375),
        "closing_projection_matrix": centred(streams_of[9], (C, C), C ** -0.5, 0.375),
        "neighbour_time_taps": centred(streams_of[10], (3, C, C), (3 * C) ** -0.5, 0.21875),
        "score_sharpness": draw_score_sharpness(jax.random.fold_in(streams_of[12], 71), part),
    }


EPSILON = 1e-05

def group_norm(values, gain):
    input_shape = values.shape
    grouped = values.reshape(input_shape[:-1] + (GROUPS, input_shape[-1] // GROUPS))
    average = lax.optimization_barrier(jnp.mean(grouped, axis=(1, 2, 4), keepdims=True))
    centered = grouped - average
    spread = lax.optimization_barrier(jnp.mean(centered * centered, axis=(1, 2, 4), keepdims=True))
    return (centered * lax.rsqrt(spread + EPSILON)).reshape(input_shape) * gain

def spatial_conv(active, weight):
    height = active.shape[1]
    breadth = active.shape[2]
    channels = active.shape[3]
    padded = jnp.pad(active, ((0, 0), (1, 1), (1, 1), (0, 0)))
    total = jnp.zeros((active.shape[0] * height * breadth, channels), jnp.float32)
    for row_tap in range(3):
        for col_tap in range(3):
            window = padded[:, row_tap:row_tap + height, col_tap:col_tap + breadth, :].reshape(-1, channels)
            total = total + jnp.dot(window, weight[row_tap, col_tap], preferred_element_type=jnp.float32)
    return total.reshape(active.shape)

def spatial_block(latent_images, initial_group_scale, initial_conv_taps, later_group_scale, later_conv_taps):
    first = jax.nn.silu(group_norm(latent_images.astype(jnp.float32), initial_group_scale)).astype(jnp.bfloat16)
    hidden = spatial_conv(first, initial_conv_taps)
    second = jax.nn.silu(group_norm(hidden, later_group_scale)).astype(jnp.bfloat16)
    return (latent_images.astype(jnp.float32) + spatial_conv(second, later_conv_taps)).astype(jnp.bfloat16)

def across_time_mixing(upscaling_unit_step, prenormal_scale_vector, asking_projection_matrix, matching_projection_matrix, content_projection_matrix, closing_projection_matrix, score_sharpness):
    count, pixels, channels = upscaling_unit_step.shape
    number_of_subspaces = score_sharpness.shape[0]
    subspace_dimension = channels // number_of_subspaces
    widened = upscaling_unit_step.astype(jnp.float32)
    average = lax.optimization_barrier(jnp.mean(widened, axis=-1, keepdims=True))
    centered = widened - average
    spread = lax.optimization_barrier(jnp.mean(centered * centered, axis=-1, keepdims=True))
    normed = (centered * lax.rsqrt(spread + EPSILON) * prenormal_scale_vector).astype(jnp.bfloat16).reshape(-1, channels)

    def project(weight):
        return jnp.dot(normed, weight, preferred_element_type=jnp.float32).astype(jnp.bfloat16).reshape(count, pixels, number_of_subspaces, subspace_dimension)
    queries = project(asking_projection_matrix)
    keys = project(matching_projection_matrix)
    values = project(content_projection_matrix)
    raw_pair_scores = jnp.einsum('fphd,gphd->phfg', queries.astype(jnp.float32), keys.astype(jnp.float32))
    raw_pair_scores = raw_pair_scores * (score_sharpness / math.sqrt(subspace_dimension))[None, :, None, None]
    probs = jax.nn.softmax(raw_pair_scores, axis=-1).astype(jnp.bfloat16)
    attended = jnp.einsum('phfg,gphd->fphd', probs.astype(jnp.float32), values.astype(jnp.float32))
    attended = attended.astype(jnp.bfloat16).reshape(-1, channels)
    output = widened + jnp.dot(attended, closing_projection_matrix, preferred_element_type=jnp.float32).reshape(upscaling_unit_step.shape)
    return output.astype(jnp.bfloat16)

def time_mix(padded, weight):
    count = padded.shape[0] - 2
    channels = padded.shape[-1]
    center = padded[1:count + 1]
    total = center.astype(jnp.float32).reshape(-1, channels)
    for offset in range(3):
        total = total + jnp.dot(padded[offset:offset + count].reshape(-1, channels), weight[offset], preferred_element_type=jnp.float32)
    return total.reshape(center.shape).astype(jnp.bfloat16)

def reference(latent_images, initial_group_scale, initial_conv_taps, later_group_scale, later_conv_taps, prenormal_scale_vector, asking_projection_matrix, matching_projection_matrix, content_projection_matrix, closing_projection_matrix, neighbour_time_taps, score_sharpness):

    def one_frame(single):
        return spatial_block(single[None], initial_group_scale, initial_conv_taps, later_group_scale, later_conv_taps)[0]
    spatial = lax.map(one_frame, latent_images)
    blocks = spatial.reshape(FRAMES, N_FRAME, OWN, C).transpose(1, 0, 2, 3)

    def owner(upscaling_unit_step):
        mixed_result_tensor = across_time_mixing(upscaling_unit_step, prenormal_scale_vector, asking_projection_matrix, matching_projection_matrix, content_projection_matrix, closing_projection_matrix, score_sharpness)
        return time_mix(jnp.pad(mixed_result_tensor, ((1, 1), (0, 0), (0, 0))), neighbour_time_taps)
    finished = lax.map(owner, blocks)
    return finished.transpose(1, 0, 2, 3).reshape(FRAMES, HT, W, C)
```

```python
import functools
import math

import jax
import jax.numpy as jnp
from jax import lax
from jax.experimental import pallas as pl
from jax.experimental.pallas import tpu as pltpu
from jax.sharding import PartitionSpec as P

GROUPS = 32
EPSILON = 1e-05
SUB = 8
CHUNK = 16
F32 = jnp.float32
BF16 = jnp.bfloat16


def dot(a, b):
    return jnp.dot(a, b, preferred_element_type=F32)


def kernel(
    n,
    per,
    height,
    width,
    own,
    heads,
    x_ref,
    g1_ref,
    w1_ref,
    g2_ref,
    w2_ref,
    pn_ref,
    wq_ref,
    wk_ref,
    wv_ref,
    wo_ref,
    tt_ref,
    sharp_ref,
    out_ref,
    act,
    hid,
    local,
    recv,
    q_s,
    k_s,
    v_s,
    o_s,
    fin,
    back,
    send1,
    recv1,
    send2,
    recv2,
):
    me = lax.axis_index("frame")
    pixels = height * width
    channels = x_ref.shape[-1]
    frames = n * per
    padded = local.shape[2]
    chunks = padded // CHUNK
    rows = frames * SUB
    block = min(rows, 256)

    def peer(j):
        t = (j + 1) // 2
        k = n // 2 + (1 - 2 * (j % 2)) * t
        return lax.rem(me + k, n), lax.rem(me - k + n, n)

    barrier = pltpu.get_barrier_semaphore()

    @pl.loop(0, n - 1)
    def _(j):
        to, _ = peer(j)
        pl.semaphore_signal(
            barrier, inc=1, device_id={"frame": to}, device_id_type=pl.DeviceIdType.MESH
        )

    act[pl.ds(0, width), :] = jnp.zeros((width, 3 * channels), BF16)
    act[pl.ds((height + 1) * width, width), :] = jnp.zeros((width, 3 * channels), BF16)

    ci = lax.broadcasted_iota(jnp.int32, (channels, channels), 0) // (channels // GROUPS)
    cj = lax.broadcasted_iota(jnp.int32, (channels, channels), 1) // (channels // GROUPS)
    same_group = jnp.where(ci == cj, 1.0, 0.0).astype(F32)
    scale = 1.0 / (pixels * (channels // GROUPS))
    col = lax.broadcasted_iota(jnp.int32, (width, channels), 0)

    def group_mean(partial):
        total = jnp.broadcast_to(jnp.sum(partial, axis=0, keepdims=True), (8, channels))
        return (
            jnp.dot(
                total, same_group, preferred_element_type=F32, precision=lax.Precision.HIGHEST
            )[:1]
            * scale
        )

    def row_of(i):
        return pl.ds(pl.multiple_of(i * width, width), width)

    def fold(v):
        return jnp.sum(v.reshape(width // 8, 8, channels), axis=0)

    def norm_silu(load, gain):
        zero = jnp.zeros((8, channels), F32)
        mean = group_mean(
            lax.fori_loop(0, height, lambda i, s: s + fold(load(i)), zero)
        )

        def square(i, s):
            c = load(i) - mean
            return s + fold(c * c)

        inv = lax.rsqrt(group_mean(lax.fori_loop(0, height, square, zero)) + EPSILON)

        @pl.loop(0, height)
        def _(i):
            v = (load(i) - mean) * inv * gain
            y = (v / (1.0 + jnp.exp(-v))).astype(BF16)
            wide = y.astype(F32)
            there = pl.ds(pl.multiple_of((i + 1) * width, width), width)
            act[there, pl.ds(0, channels)] = jnp.where(
                col == 0, 0.0, pltpu.roll(wide, 1, 0)
            ).astype(BF16)
            act[there, pl.ds(channels, channels)] = y
            act[there, pl.ds(2 * channels, channels)] = jnp.where(
                col == width - 1, 0.0, pltpu.roll(wide, width - 1, 0)
            ).astype(BF16)

    def conv(w_ref):
        total = None
        for a in range(3):
            term = dot(
                act[pl.ds(a * width, pixels), :],
                w_ref[pl.ds(a * 3 * channels, 3 * channels), :],
            )
            total = term if total is None else total + term
        return total

    def forward(f, to, source):
        return pltpu.make_async_remote_copy(
            src_ref=local.at[f, to],
            dst_ref=recv.at[source * per + f],
            send_sem=send1.at[f, to],
            recv_sem=recv1.at[f, source],
            device_id={"frame": to},
            device_id_type=pl.DeviceIdType.MESH,
        )

    @pl.loop(0, per)
    def _(f):
        norm_silu(lambda i: x_ref[f, row_of(i), :].astype(F32), g1_ref[...])
        hid[...] = conv(w1_ref)
        norm_silu(lambda i: hid[row_of(i), :], g2_ref[...])
        hid[...] = x_ref[f].astype(F32) + conv(w2_ref)
        for o in range(n):
            v = hid[pl.ds(o * own, own), :]
            if padded > own:
                v = jnp.concatenate([v, jnp.zeros((padded - own, channels), F32)], axis=0)
            local[f, o] = v.astype(BF16)
        recv[me * per + f] = local[f, me]

        @pl.when(f == 0)
        def _():
            pl.semaphore_wait(barrier, n - 1)

        @pl.loop(0, n - 1)
        def _(j):
            to, _ = peer(j)
            forward(f, to, me).start()

    @pl.loop(0, per)
    def _(f):
        @pl.loop(0, n - 1)
        def _(j):
            to, source = peer(j)
            forward(f, to, source).wait_recv()

    lane = lax.broadcasted_iota(jnp.int32, (1, channels), 1) // (channels // heads)
    ri = lax.broadcasted_iota(jnp.int32, (block, rows), 0) % SUB
    rj = lax.broadcasted_iota(jnp.int32, (block, rows), 1) % SUB
    same_pixel = ri == rj
    halves = CHUNK // SUB

    def returning(g, to, source):
        px = pl.ds(pl.multiple_of(g * CHUNK, CHUNK), CHUNK)
        return pltpu.make_async_remote_copy(
            src_ref=fin.at[to, :, px],
            dst_ref=back.at[source, :, px],
            send_sem=send2.at[g, to],
            recv_sem=recv2.at[g, source],
            device_id={"frame": to},
            device_id_type=pl.DeviceIdType.MESH,
        )

    @pl.loop(0, chunks)
    def _(g):
        px = pl.ds(pl.multiple_of(g * CHUNK, CHUNK), CHUNK)
        x = recv[:, px, :].astype(F32).reshape(frames * CHUNK, channels)
        c = x - jnp.mean(x, axis=-1, keepdims=True)
        var = jnp.mean(c * c, axis=-1, keepdims=True)
        normed = (c * lax.rsqrt(var + EPSILON) * pn_ref[...]).astype(BF16)
        for ref, w in ((q_s, wq_ref), (k_s, wk_ref), (v_s, wv_ref)):
            t = dot(normed, w[...]).reshape(frames, CHUNK, channels)
            for half in range(halves):
                ref[half] = (
                    t[:, half * SUB : (half + 1) * SUB].reshape(rows, channels).astype(BF16)
                )

        @pl.loop(0, halves)
        def _(half):
            @pl.loop(0, rows // block)
            def _(b):
                qs = pl.ds(pl.multiple_of(b * block, block), block)
                q = q_s[half, qs, :]
                k = k_s[half]
                v = v_s[half]
                total = None
                for h in range(heads):
                    keep = jnp.where(lane == h, 1.0, 0.0).astype(BF16)
                    s = lax.dot_general(
                        q * keep, k, (((1,), (1,)), ((), ())), preferred_element_type=F32
                    )
                    s = s * (sharp_ref[h] * (1.0 / math.sqrt(channels // heads)))
                    s = jnp.where(same_pixel, s, -jnp.inf)
                    e = jnp.exp(s - jnp.max(s, axis=-1, keepdims=True))
                    p = (e * (1.0 / jnp.sum(e, axis=-1, keepdims=True))).astype(BF16)
                    term = dot(p, v * keep)
                    total = term if total is None else total + term
                o_s[half, qs, :] = total

        attended = jnp.concatenate(
            [o_s[half].reshape(frames, SUB, channels) for half in range(halves)], axis=1
        )
        attended = attended.reshape(frames * CHUNK, channels).astype(BF16)
        x = recv[:, px, :].astype(F32).reshape(frames * CHUNK, channels)
        mixed = (x + dot(attended, wo_ref[...])).astype(BF16)
        edge = jnp.zeros((CHUNK, channels), BF16)
        before = jnp.concatenate([edge, mixed[:-CHUNK]], axis=0)
        after = jnp.concatenate([mixed[CHUNK:], edge], axis=0)
        result = mixed.astype(F32)
        for t, m in enumerate((before, mixed, after)):
            result = result + dot(m, tt_ref[t])
        fin[:, :, px, :] = result.astype(BF16).reshape(n, per, CHUNK, channels)
        back[me, :, px, :] = fin[me, :, px, :]

        @pl.loop(0, n - 1)
        def _(j):
            to, _ = peer(j)
            returning(g, to, me).start()

    @pl.loop(0, chunks)
    def _(g):
        @pl.loop(0, n - 1)
        def _(j):
            to, source = peer(j)
            returning(g, to, source).wait_recv()

    for f in range(per):
        for o in range(n):
            hid[pl.ds(o * own, own), :] = back[o, f].astype(F32)[:own]
        out_ref[f] = hid[...].astype(BF16)

    @pl.loop(0, n - 1)
    def _(j):
        to, source = peer(j)

        @pl.loop(0, per)
        def _(f):
            forward(f, to, source).wait_send()

        @pl.loop(0, chunks)
        def _(g):
            returning(g, to, source).wait_send()


def on_device(n, latent, g1, w1, g2, w2, pn, wq, wk, wv, wo, tt, sharp):
    per, height, width, channels = latent.shape
    pixels = height * width
    own = pixels // n
    padded = -(-own // CHUNK) * CHUNK
    frames = n * per
    heads = sharp.shape[0]
    rows = frames * SUB
    halves = CHUNK // SUB
    chunks = padded // CHUNK
    vmem = pl.BlockSpec(memory_space=pltpu.VMEM)
    out = pl.pallas_call(
        functools.partial(kernel, n, per, height, width, own, heads),
        out_shape=jax.ShapeDtypeStruct((per, pixels, channels), BF16),
        in_specs=[vmem] * 11 + [pl.BlockSpec(memory_space=pltpu.SMEM)],
        out_specs=vmem,
        scratch_shapes=[
            pltpu.VMEM(((height + 2) * width, 3 * channels), BF16),
            pltpu.VMEM((pixels, channels), F32),
            pltpu.VMEM((per, n, padded, channels), BF16),
            pltpu.VMEM((frames, padded, channels), BF16),
            pltpu.VMEM((halves, rows, channels), BF16),
            pltpu.VMEM((halves, rows, channels), BF16),
            pltpu.VMEM((halves, rows, channels), BF16),
            pltpu.VMEM((halves, rows, channels), F32),
            pltpu.VMEM((n, per, padded, channels), BF16),
            pltpu.VMEM((n, per, padded, channels), BF16),
            pltpu.SemaphoreType.DMA((per, n)),
            pltpu.SemaphoreType.DMA((per, n)),
            pltpu.SemaphoreType.DMA((chunks, n)),
            pltpu.SemaphoreType.DMA((chunks, n)),
        ],
        compiler_params=pltpu.CompilerParams(
            collective_id=0, has_side_effects=True, vmem_limit_bytes=60 * 1024 * 1024
        ),
        name="block",
    )(
        latent.reshape(per, pixels, channels),
        g1.reshape(1, channels),
        w1.reshape(9 * channels, channels),
        g2.reshape(1, channels),
        w2.reshape(9 * channels, channels),
        pn.reshape(1, channels),
        wq,
        wk,
        wv,
        wo,
        tt,
        sharp,
    )
    return out.reshape(latent.shape)


def solution(mesh):
    split = P(("groups", "frame"), None, None, None)
    return jax.shard_map(
        functools.partial(on_device, mesh.shape["frame"]),
        mesh=mesh,
        in_specs=(split,) + (P(),) * 11,
        out_specs=split,
        check_vma=False,
    )
```

```python
import functools
import math

import jax
import jax.numpy as jnp
from jax import lax
from jax.experimental import pallas as pl
from jax.experimental.pallas import tpu as pltpu
from jax.sharding import PartitionSpec as P

GROUPS = 32
EPSILON = 1e-05
SUB = 8
CHUNK = 16
PAIR = 2
F32 = jnp.float32
BF16 = jnp.bfloat16


def dot(a, b):
    return jnp.dot(a, b, preferred_element_type=F32)


def kernel(
    n,
    per,
    height,
    width,
    heads,
    x_hbm,
    g1_ref,
    w1_hbm,
    g2_ref,
    w2_hbm,
    pn_ref,
    wq_hbm,
    wk_hbm,
    wv_hbm,
    wo_hbm,
    tt_hbm,
    sharp_ref,
    out_ref,
    x_ref,
    w1_ref,
    w2_ref,
    wq_ref,
    wk_ref,
    wv_ref,
    wo_ref,
    tt_ref,
    act,
    hid,
    local,
    recv,
    q_s,
    k_s,
    v_s,
    o_s,
    fin,
    load,
    keep_sem,
    send1,
    recv1,
    send2,
    recv2,
):
    me = lax.axis_index("frame")
    pixels = height * width
    channels = x_ref.shape[-1]
    frames = n * per
    units = pixels // CHUNK
    chunks = -(-units // n)
    missing = chunks * n - units
    rows = frames * SUB
    block = min(rows, 256)

    def peer(j):
        t = (j + 1) // 2
        k = n // 2 + (1 - 2 * (j % 2)) * t
        return lax.rem(me + k, n), lax.rem(me - k + n, n)

    def count(g):
        return n - missing * (g // (chunks - 1) if chunks > 1 else 1)

    def rows_of(g, o):
        unit = g * n + (o * count(g)) // n
        return pl.ds(pl.multiple_of(unit * CHUNK, CHUNK), CHUNK)

    def owns(g, o):
        return ((o + 1) * count(g)) // n > (o * count(g)) // n

    loads = [pltpu.make_async_copy(x_hbm.at[f], x_ref.at[f], load.at[f]) for f in range(per)]
    for source, target in (
        (w1_hbm, w1_ref),
        (w2_hbm, w2_ref),
        (wq_hbm, wq_ref),
        (wk_hbm, wk_ref),
        (wv_hbm, wv_ref),
        (wo_hbm, wo_ref),
        (tt_hbm, tt_ref),
    ):
        loads.append(pltpu.make_async_copy(source, target, load.at[len(loads)]))
    loads = [loads[0], loads[per]] + loads[1:per] + loads[per + 1 :]
    for copy in loads:
        copy.start()

    barrier = pltpu.get_barrier_semaphore()

    @pl.loop(0, n - 1)
    def _(j):
        to, _ = peer(j)
        pl.semaphore_signal(
            barrier, inc=1, device_id={"frame": to}, device_id_type=pl.DeviceIdType.MESH
        )

    act[pl.ds(0, width), :] = jnp.zeros((width, 3 * channels), BF16)
    act[pl.ds((height + 1) * width, width), :] = jnp.zeros((width, 3 * channels), BF16)

    ci = lax.broadcasted_iota(jnp.int32, (channels, channels), 0) // (channels // GROUPS)
    cj = lax.broadcasted_iota(jnp.int32, (channels, channels), 1) // (channels // GROUPS)
    same_group = jnp.where(ci == cj, 1.0, 0.0).astype(F32)
    scale = 1.0 / (pixels * (channels // GROUPS))
    col = lax.broadcasted_iota(jnp.int32, (width, channels), 0)

    def group_mean(partial):
        total = jnp.broadcast_to(jnp.sum(partial, axis=0, keepdims=True), (8, channels))
        return (
            jnp.dot(
                total, same_group, preferred_element_type=F32, precision=lax.Precision.HIGHEST
            )[:1]
            * scale
        )

    def row_of(i):
        return pl.ds(pl.multiple_of(i * width, width), width)

    def fold(v):
        return jnp.sum(v.reshape(width // 8, 8, channels), axis=0)

    def norm_silu(load, gain):
        zero = jnp.zeros((8, channels), F32)
        mean = group_mean(
            lax.fori_loop(0, height, lambda i, s: s + fold(load(i)), zero)
        )

        def square(i, s):
            c = load(i) - mean
            return s + fold(c * c)

        inv = lax.rsqrt(group_mean(lax.fori_loop(0, height, square, zero)) + EPSILON)

        @pl.loop(0, height)
        def _(i):
            v = (load(i) - mean) * inv * gain
            y = (v / (1.0 + jnp.exp(-v))).astype(BF16)
            wide = y.astype(F32)
            there = pl.ds(pl.multiple_of((i + 1) * width, width), width)
            act[there, pl.ds(0, channels)] = jnp.where(
                col == 0, 0.0, pltpu.roll(wide, 1, 0)
            ).astype(BF16)
            act[there, pl.ds(channels, channels)] = y
            act[there, pl.ds(2 * channels, channels)] = jnp.where(
                col == width - 1, 0.0, pltpu.roll(wide, width - 1, 0)
            ).astype(BF16)

    def conv(w_ref, start, size):
        total = None
        for a in range(3):
            term = dot(
                act[pl.ds(a * width + start, size), :],
                w_ref[pl.ds(a * 3 * channels, 3 * channels), :],
            )
            total = term if total is None else total + term
        return total

    def forward(f, g, to, source):
        return pltpu.make_async_remote_copy(
            src_ref=local.at[f, rows_of(g, to)],
            dst_ref=recv.at[g, source * per + f],
            send_sem=send1.at[f, g, to],
            recv_sem=recv1.at[f, g, source],
            device_id={"frame": to},
            device_id_type=pl.DeviceIdType.MESH,
        )

    loads[0].wait()

    @pl.loop(0, per)
    def _(f):
        norm_silu(lambda i: x_ref[f, row_of(i), :].astype(F32), g1_ref[...])

        @pl.when(f == 0)
        def _():
            loads[1].wait()

        hid[...] = conv(w1_ref, 0, pixels)
        norm_silu(lambda i: hid[row_of(i), :], g2_ref[...])

        @pl.when(f == 0)
        def _():
            for copy in loads[2:]:
                copy.wait()
            pl.semaphore_wait(barrier, n - 1)

        for first in range(0, chunks, PAIR):
            last = min(first + PAIR, chunks)
            start = first * n * CHUNK
            size = min(last * n * CHUNK, pixels) - start
            part = pl.ds(start, size)
            local[f, part, :] = (x_ref[f, part, :].astype(F32) + conv(w2_ref, start, size)).astype(
                BF16
            )

            @pl.loop(first, last)
            def _(g):
                @pl.loop(0, n - 1)
                def _(j):
                    to, _ = peer(j)

                    @pl.when(owns(g, to))
                    def _():
                        forward(f, g, to, me).start()

                @pl.when(owns(g, me))
                def _():
                    recv[g, me * per + f] = local[f, rows_of(g, me), :]

    lane = lax.broadcasted_iota(jnp.int32, (1, channels), 1) // (channels // heads)
    ri = lax.broadcasted_iota(jnp.int32, (block, rows), 0) % SUB
    rj = lax.broadcasted_iota(jnp.int32, (block, rows), 1) % SUB
    same_pixel = ri == rj
    halves = CHUNK // SUB

    def returning(g, to, source):
        return pltpu.make_async_remote_copy(
            src_ref=fin.at[g, to],
            dst_ref=out_ref.at[:, rows_of(g, source)],
            send_sem=send2.at[g, to],
            recv_sem=recv2.at[g, source],
            device_id={"frame": to},
            device_id_type=pl.DeviceIdType.MESH,
        )

    def keeping(g):
        return pltpu.make_async_copy(
            fin.at[g, me], out_ref.at[:, rows_of(g, me)], keep_sem.at[g]
        )

    def attend(g):
        @pl.loop(0, per)
        def _(f):
            @pl.loop(0, n - 1)
            def _(j):
                to, source = peer(j)
                forward(f, g, to, source).wait_recv()

        x = recv[g].astype(F32).reshape(frames * CHUNK, channels)
        c = x - jnp.mean(x, axis=-1, keepdims=True)
        var = jnp.mean(c * c, axis=-1, keepdims=True)
        normed = (c * lax.rsqrt(var + EPSILON) * pn_ref[...]).astype(BF16)
        for ref, w in ((q_s, wq_ref), (k_s, wk_ref), (v_s, wv_ref)):
            t = dot(normed, w[...]).reshape(frames, CHUNK, channels)
            for half in range(halves):
                ref[half] = (
                    t[:, half * SUB : (half + 1) * SUB].reshape(rows, channels).astype(BF16)
                )

        @pl.loop(0, halves)
        def _(half):
            @pl.loop(0, rows // block)
            def _(b):
                qs = pl.ds(pl.multiple_of(b * block, block), block)
                q = q_s[half, qs, :]
                k = k_s[half]
                v = v_s[half]
                total = None
                for h in range(heads):
                    keep = jnp.where(lane == h, 1.0, 0.0).astype(BF16)
                    s = lax.dot_general(
                        q * keep, k, (((1,), (1,)), ((), ())), preferred_element_type=F32
                    )
                    s = s * (sharp_ref[h] * (1.0 / math.sqrt(channels // heads)))
                    s = jnp.where(same_pixel, s, -jnp.inf)
                    e = jnp.exp(s - jnp.max(s, axis=-1, keepdims=True))
                    p = (e * (1.0 / jnp.sum(e, axis=-1, keepdims=True))).astype(BF16)
                    term = dot(p, v * keep)
                    total = term if total is None else total + term
                o_s[half, qs, :] = total

        attended = jnp.concatenate(
            [o_s[half].reshape(frames, SUB, channels) for half in range(halves)], axis=1
        )
        attended = attended.reshape(frames * CHUNK, channels).astype(BF16)
        x = recv[g].astype(F32).reshape(frames * CHUNK, channels)
        mixed = (x + dot(attended, wo_ref[...])).astype(BF16)
        edge = jnp.zeros((CHUNK, channels), BF16)
        before = jnp.concatenate([edge, mixed[:-CHUNK]], axis=0)
        after = jnp.concatenate([mixed[CHUNK:], edge], axis=0)
        result = mixed.astype(F32)
        for t, m in enumerate((before, mixed, after)):
            result = result + dot(m, tt_ref[t])
        fin[g] = result.astype(BF16).reshape(n, per, CHUNK, channels)
        keeping(g).start()

        @pl.loop(0, n - 1)
        def _(j):
            to, _ = peer(j)
            returning(g, to, me).start()

    @pl.loop(0, chunks)
    def _(g):
        @pl.when(owns(g, me))
        def _():
            attend(g)

    @pl.loop(0, chunks)
    def _(g):
        @pl.when(owns(g, me))
        def _():
            keeping(g).wait()

        @pl.loop(0, n - 1)
        def _(j):
            to, source = peer(j)

            @pl.when(owns(g, source))
            def _():
                returning(g, to, source).wait_recv()

            @pl.when(owns(g, me))
            def _():
                returning(g, to, source).wait_send()

            @pl.when(owns(g, to))
            def _():
                @pl.loop(0, per)
                def _(f):
                    forward(f, g, to, source).wait_send()


def on_device(n, latent, g1, w1, g2, w2, pn, wq, wk, wv, wo, tt, sharp):
    per, height, width, channels = latent.shape
    pixels = height * width
    frames = n * per
    heads = sharp.shape[0]
    rows = frames * SUB
    halves = CHUNK // SUB
    chunks = -(-(pixels // CHUNK) // n)
    vmem = pl.BlockSpec(memory_space=pltpu.VMEM)
    hbm = pl.BlockSpec(memory_space=pl.ANY)
    out = pl.pallas_call(
        functools.partial(kernel, n, per, height, width, heads),
        out_shape=jax.ShapeDtypeStruct((per, pixels, channels), BF16),
        in_specs=[hbm, vmem, hbm, vmem, hbm, vmem]
        + [hbm] * 5
        + [pl.BlockSpec(memory_space=pltpu.SMEM)],
        out_specs=hbm,
        scratch_shapes=[
            pltpu.VMEM((per, pixels, channels), BF16),
            pltpu.VMEM((9 * channels, channels), BF16),
            pltpu.VMEM((9 * channels, channels), BF16),
            pltpu.VMEM(wq.shape, BF16),
            pltpu.VMEM(wk.shape, BF16),
            pltpu.VMEM(wv.shape, BF16),
            pltpu.VMEM(wo.shape, BF16),
            pltpu.VMEM(tt.shape, BF16),
            pltpu.VMEM(((height + 2) * width, 3 * channels), BF16),
            pltpu.VMEM((pixels, channels), F32),
            pltpu.VMEM((per, pixels, channels), BF16),
            pltpu.VMEM((chunks, frames, CHUNK, channels), BF16),
            pltpu.VMEM((halves, rows, channels), BF16),
            pltpu.VMEM((halves, rows, channels), BF16),
            pltpu.VMEM((halves, rows, channels), BF16),
            pltpu.VMEM((halves, rows, channels), F32),
            pltpu.VMEM((chunks, n, per, CHUNK, channels), BF16),
            pltpu.SemaphoreType.DMA((per + 7,)),
            pltpu.SemaphoreType.DMA((chunks,)),
            pltpu.SemaphoreType.DMA((per, chunks, n)),
            pltpu.SemaphoreType.DMA((per, chunks, n)),
            pltpu.SemaphoreType.DMA((chunks, n)),
            pltpu.SemaphoreType.DMA((chunks, n)),
        ],
        compiler_params=pltpu.CompilerParams(
            collective_id=0, has_side_effects=True, vmem_limit_bytes=60 * 1024 * 1024
        ),
        name="block",
    )(
        latent.reshape(per, pixels, channels),
        g1.reshape(1, channels),
        w1.reshape(9 * channels, channels),
        g2.reshape(1, channels),
        w2.reshape(9 * channels, channels),
        pn.reshape(1, channels),
        wq,
        wk,
        wv,
        wo,
        tt,
        sharp,
    )
    return out.reshape(latent.shape)


def solution(mesh):
    split = P(("groups", "frame"), None, None, None)
    return jax.shard_map(
        functools.partial(on_device, mesh.shape["frame"]),
        mesh=mesh,
        in_specs=(split,) + (P(),) * 11,
        out_specs=split,
        check_vma=False,
    )
```

```python
import functools
import math

import jax
import jax.numpy as jnp
from jax import lax
from jax.experimental import pallas as pl
from jax.experimental.pallas import tpu as pltpu
from jax.sharding import PartitionSpec as P

GROUPS = 32
EPSILON = 1e-05
SUB = 8
CHUNK = 16
PAIR = 1
F32 = jnp.float32
BF16 = jnp.bfloat16


def dot(a, b):
    return jnp.dot(a, b, preferred_element_type=F32)


def kernel(
    n,
    per,
    height,
    width,
    heads,
    x_hbm,
    g1_ref,
    w1_hbm,
    g2_ref,
    w2_hbm,
    pn_ref,
    wq_hbm,
    wk_hbm,
    wv_hbm,
    wo_hbm,
    tt_hbm,
    sharp_ref,
    out_ref,
    x_ref,
    w1_ref,
    w2_ref,
    wq_ref,
    wk_ref,
    wv_ref,
    wo_ref,
    tt_ref,
    act,
    hid,
    local,
    recv,
    q_s,
    k_s,
    v_s,
    o_s,
    fin,
    load,
    keep_sem,
    send1,
    recv1,
    send2,
    recv2,
):
    me = lax.axis_index("frame")
    pixels = height * width
    channels = x_ref.shape[-1]
    frames = n * per
    units = pixels // CHUNK
    chunks = -(-units // n)
    missing = chunks * n - units
    rows = frames * SUB
    block = min(rows, 256)

    def peer(j):
        t = (j + 1) // 2
        k = n // 2 + (1 - 2 * (j % 2)) * t
        return lax.rem(me + k, n), lax.rem(me - k + n, n)

    def count(g):
        return n - missing * (g // (chunks - 1) if chunks > 1 else 1)

    def rows_of(g, o):
        unit = g * n + (o * count(g)) // n
        return pl.ds(pl.multiple_of(unit * CHUNK, CHUNK), CHUNK)

    def owns(g, o):
        return ((o + 1) * count(g)) // n > (o * count(g)) // n

    loads = [pltpu.make_async_copy(x_hbm.at[f], x_ref.at[f], load.at[f]) for f in range(per)]
    for source, target in (
        (w1_hbm, w1_ref),
        (w2_hbm, w2_ref),
        (wq_hbm, wq_ref),
        (wk_hbm, wk_ref),
        (wv_hbm, wv_ref),
        (wo_hbm, wo_ref),
        (tt_hbm, tt_ref),
    ):
        loads.append(pltpu.make_async_copy(source, target, load.at[len(loads)]))
    loads = [loads[0], loads[per]] + loads[1:per] + loads[per + 1 :]
    for copy in loads:
        copy.start()

    barrier = pltpu.get_barrier_semaphore()

    @pl.loop(0, n - 1)
    def _(j):
        to, _ = peer(j)
        pl.semaphore_signal(
            barrier, inc=1, device_id={"frame": to}, device_id_type=pl.DeviceIdType.MESH
        )

    act[pl.ds(0, width), :] = jnp.zeros((width, 3 * channels), BF16)
    act[pl.ds((height + 1) * width, width), :] = jnp.zeros((width, 3 * channels), BF16)

    place = lax.broadcasted_iota(jnp.int32, (8, channels), 1)
    scale = 1.0 / (pixels * (channels // GROUPS))
    col = lax.broadcasted_iota(jnp.int32, (width, channels), 0)

    def group_mean(partial):
        total = jnp.broadcast_to(jnp.sum(partial, axis=0, keepdims=True), (8, channels))
        step = 1
        while step < channels // GROUPS:
            total = total + jnp.where(
                (place // step) % 2 == 0,
                pltpu.roll(total, channels - step, 1),
                pltpu.roll(total, step, 1),
            )
            step *= 2
        return total[:1] * scale

    def row_of(i):
        return pl.ds(pl.multiple_of(i * width, width), width)

    def fold(v):
        return jnp.sum(v.reshape(width // 8, 8, channels), axis=0)

    def norm_silu(load, gain):
        zero = jnp.zeros((8, channels), F32)
        mean = group_mean(
            lax.fori_loop(0, height, lambda i, s: s + fold(load(i)), zero)
        )

        def square(i, s):
            c = load(i) - mean
            return s + fold(c * c)

        inv = lax.rsqrt(group_mean(lax.fori_loop(0, height, square, zero)) + EPSILON)

        @pl.loop(0, height)
        def _(i):
            v = (load(i) - mean) * inv * gain
            y = (0.5 * v * (1.0 + jnp.tanh(0.5 * v))).astype(BF16)
            wide = y.astype(F32)
            there = pl.ds(pl.multiple_of((i + 1) * width, width), width)
            act[there, pl.ds(0, channels)] = jnp.where(
                col == 0, 0.0, pltpu.roll(wide, 1, 0)
            ).astype(BF16)
            act[there, pl.ds(channels, channels)] = y
            act[there, pl.ds(2 * channels, channels)] = jnp.where(
                col == width - 1, 0.0, pltpu.roll(wide, width - 1, 0)
            ).astype(BF16)

    def conv(w_ref, start, size):
        total = None
        for a in range(3):
            term = dot(
                act[pl.ds(a * width + start, size), :],
                w_ref[pl.ds(a * 3 * channels, 3 * channels), :],
            )
            total = term if total is None else total + term
        return total

    def forward(f, g, to, source):
        return pltpu.make_async_remote_copy(
            src_ref=local.at[f, rows_of(g, to)],
            dst_ref=recv.at[g, source * per + f],
            send_sem=send1.at[f, g, to],
            recv_sem=recv1.at[f, g, source],
            device_id={"frame": to},
            device_id_type=pl.DeviceIdType.MESH,
        )

    loads[0].wait()

    @pl.loop(0, per)
    def _(f):
        norm_silu(lambda i: x_ref[f, row_of(i), :].astype(F32), g1_ref[...])

        @pl.when(f == 0)
        def _():
            loads[1].wait()

        hid[...] = conv(w1_ref, 0, pixels)
        norm_silu(lambda i: hid[row_of(i), :], g2_ref[...])

        @pl.when(f == 0)
        def _():
            for copy in loads[2:]:
                copy.wait()
            pl.semaphore_wait(barrier, n - 1)

        for first in range(0, chunks, PAIR):
            last = min(first + PAIR, chunks)
            start = first * n * CHUNK
            size = min(last * n * CHUNK, pixels) - start
            part = pl.ds(start, size)
            local[f, part, :] = (x_ref[f, part, :].astype(F32) + conv(w2_ref, start, size)).astype(
                BF16
            )

            @pl.loop(first, last)
            def _(g):
                @pl.loop(0, n - 1)
                def _(j):
                    to, _ = peer(j)

                    @pl.when(owns(g, to))
                    def _():
                        forward(f, g, to, me).start()

                @pl.when(owns(g, me))
                def _():
                    recv[g, me * per + f] = local[f, rows_of(g, me), :]

    lane = lax.broadcasted_iota(jnp.int32, (1, channels), 1) // (channels // heads)
    ri = lax.broadcasted_iota(jnp.int32, (block, rows), 0) % SUB
    rj = lax.broadcasted_iota(jnp.int32, (block, rows), 1) % SUB
    same_pixel = ri == rj
    halves = CHUNK // SUB

    def returning(g, to, source):
        return pltpu.make_async_remote_copy(
            src_ref=fin.at[g, to],
            dst_ref=out_ref.at[:, rows_of(g, source)],
            send_sem=send2.at[g, to],
            recv_sem=recv2.at[g, source],
            device_id={"frame": to},
            device_id_type=pl.DeviceIdType.MESH,
        )

    def keeping(g):
        return pltpu.make_async_copy(
            fin.at[g, me], out_ref.at[:, rows_of(g, me)], keep_sem.at[g]
        )

    def attend(g):
        @pl.loop(0, per)
        def _(f):
            @pl.loop(0, n - 1)
            def _(j):
                to, source = peer(j)
                forward(f, g, to, source).wait_recv()

        x = recv[g].astype(F32).reshape(frames * CHUNK, channels)
        c = x - jnp.mean(x, axis=-1, keepdims=True)
        var = jnp.mean(c * c, axis=-1, keepdims=True)
        normed = (c * lax.rsqrt(var + EPSILON) * pn_ref[...]).astype(BF16)
        for ref, w in ((q_s, wq_ref), (k_s, wk_ref), (v_s, wv_ref)):
            t = dot(normed, w[...]).reshape(frames, CHUNK, channels)
            for half in range(halves):
                ref[half] = (
                    t[:, half * SUB : (half + 1) * SUB].reshape(rows, channels).astype(BF16)
                )

        @pl.loop(0, halves)
        def _(half):
            @pl.loop(0, rows // block)
            def _(b):
                qs = pl.ds(pl.multiple_of(b * block, block), block)
                q = q_s[half, qs, :]
                k = k_s[half]
                v = v_s[half]
                total = None
                for h in range(heads):
                    keep = jnp.where(lane == h, 1.0, 0.0).astype(BF16)
                    s = lax.dot_general(
                        q * keep, k, (((1,), (1,)), ((), ())), preferred_element_type=F32
                    )
                    s = s * (sharp_ref[h] * (1.0 / math.sqrt(channels // heads)))
                    s = jnp.where(same_pixel, s, -jnp.inf)
                    e = jnp.exp(s - jnp.max(s, axis=-1, keepdims=True))
                    p = (e * (1.0 / jnp.sum(e, axis=-1, keepdims=True))).astype(BF16)
                    term = dot(p, v * keep)
                    total = term if total is None else total + term
                o_s[half, qs, :] = total

        attended = jnp.concatenate(
            [o_s[half].reshape(frames, SUB, channels) for half in range(halves)], axis=1
        )
        attended = attended.reshape(frames * CHUNK, channels).astype(BF16)
        x = recv[g].astype(F32).reshape(frames * CHUNK, channels)
        mixed = (x + dot(attended, wo_ref[...])).astype(BF16)
        edge = jnp.zeros((CHUNK, channels), BF16)
        before = jnp.concatenate([edge, mixed[:-CHUNK]], axis=0)
        after = jnp.concatenate([mixed[CHUNK:], edge], axis=0)
        result = mixed.astype(F32)
        for t, m in enumerate((before, mixed, after)):
            result = result + dot(m, tt_ref[t])
        fin[g] = result.astype(BF16).reshape(n, per, CHUNK, channels)
        keeping(g).start()

        @pl.loop(0, n - 1)
        def _(j):
            to, _ = peer(j)
            returning(g, to, me).start()

    @pl.loop(0, chunks)
    def _(g):
        @pl.when(owns(g, me))
        def _():
            attend(g)

    @pl.loop(0, chunks)
    def _(g):
        @pl.when(owns(g, me))
        def _():
            keeping(g).wait()

        @pl.loop(0, n - 1)
        def _(j):
            to, source = peer(j)

            @pl.when(owns(g, source))
            def _():
                returning(g, to, source).wait_recv()

            @pl.when(owns(g, me))
            def _():
                returning(g, to, source).wait_send()

            @pl.when(owns(g, to))
            def _():
                @pl.loop(0, per)
                def _(f):
                    forward(f, g, to, source).wait_send()


def on_device(n, latent, g1, w1, g2, w2, pn, wq, wk, wv, wo, tt, sharp):
    per, height, width, channels = latent.shape
    pixels = height * width
    frames = n * per
    heads = sharp.shape[0]
    rows = frames * SUB
    halves = CHUNK // SUB
    chunks = -(-(pixels // CHUNK) // n)
    vmem = pl.BlockSpec(memory_space=pltpu.VMEM)
    hbm = pl.BlockSpec(memory_space=pl.ANY)
    out = pl.pallas_call(
        functools.partial(kernel, n, per, height, width, heads),
        out_shape=jax.ShapeDtypeStruct((per, pixels, channels), BF16),
        in_specs=[hbm, vmem, hbm, vmem, hbm, vmem]
        + [hbm] * 5
        + [pl.BlockSpec(memory_space=pltpu.SMEM)],
        out_specs=hbm,
        scratch_shapes=[
            pltpu.VMEM((per, pixels, channels), BF16),
            pltpu.VMEM((9 * channels, channels), BF16),
            pltpu.VMEM((9 * channels, channels), BF16),
            pltpu.VMEM(wq.shape, BF16),
            pltpu.VMEM(wk.shape, BF16),
            pltpu.VMEM(wv.shape, BF16),
            pltpu.VMEM(wo.shape, BF16),
            pltpu.VMEM(tt.shape, BF16),
            pltpu.VMEM(((height + 2) * width, 3 * channels), BF16),
            pltpu.VMEM((pixels, channels), F32),
            pltpu.VMEM((per, pixels, channels), BF16),
            pltpu.VMEM((chunks, frames, CHUNK, channels), BF16),
            pltpu.VMEM((halves, rows, channels), BF16),
            pltpu.VMEM((halves, rows, channels), BF16),
            pltpu.VMEM((halves, rows, channels), BF16),
            pltpu.VMEM((halves, rows, channels), F32),
            pltpu.VMEM((chunks, n, per, CHUNK, channels), BF16),
            pltpu.SemaphoreType.DMA((per + 7,)),
            pltpu.SemaphoreType.DMA((chunks,)),
            pltpu.SemaphoreType.DMA((per, chunks, n)),
            pltpu.SemaphoreType.DMA((per, chunks, n)),
            pltpu.SemaphoreType.DMA((chunks, n)),
            pltpu.SemaphoreType.DMA((chunks, n)),
        ],
        compiler_params=pltpu.CompilerParams(
            collective_id=0, has_side_effects=True, vmem_limit_bytes=60 * 1024 * 1024
        ),
        name="block",
    )(
        latent.reshape(per, pixels, channels),
        g1.reshape(1, channels),
        w1.reshape(9 * channels, channels),
        g2.reshape(1, channels),
        w2.reshape(9 * channels, channels),
        pn.reshape(1, channels),
        wq,
        wk,
        wv,
        wo,
        tt,
        sharp,
    )
    return out.reshape(latent.shape)


def solution(mesh):
    split = P(("groups", "frame"), None, None, None)
    return jax.shard_map(
        functools.partial(on_device, mesh.shape["frame"]),
        mesh=mesh,
        in_specs=(split,) + (P(),) * 11,
        out_specs=split,
        check_vma=False,
    )
```
